32 devices in a mesh: outer: 4 (over y, core), inner: 8 (over z, x).
Axes of the slice: x: 2, y: 2, z: 4, core: 2. Of those that a mesh axis runs over, the one named last changes fastest.
Arguments:
- queries: bfloat16 [4096, 2048], P(('outer', 'inner')), may hold values from -6 to 6
- keys: bfloat16 [4096, 2048], P(('outer', 'inner')), may hold values from -6 to 6
- values: bfloat16 [4096, 2048], P(('outer', 'inner')), may hold values from -6 to 6
- gain: float32 [2048], replicated, may hold values from 0.5 to 1.5
Outputs:
- attended: bfloat16 [4096, 2048], P(('outer', 'inner'))
The draws below stay inside these ranges and needn't reach their ends.
All inputs are finite; a program needn't handle non-finite values.
Results may differ from the reference program's by a relative error of at most 0.0049.
Values sent between devices are 32-bit elements; how exact they have to be, the bound alone decides.
No kernel may reach another device: no remote copies, remote signals or barrier semaphores. Data moves between devices by JAX's collectives and lax.ppermute only.
A program may use at most 64 MiB of HBM per device.

```python
import jax
import jax.numpy as jnp
from jax import lax

HEADS = 16
HEAD_DIM = 128
STRETCH = 128
TOKENS = 4096


def shard_levels(rng, shape, cuts, least, high):
    level = 1.0
    for axis_at, shards_of in cuts:
        draws = jax.random.uniform(jax.random.fold_in(jax.random.fold_in(rng, 6), axis_at), (shards_of,), jnp.float32, least / len(cuts), high / len(cuts))
        level = level * jnp.repeat(jnp.exp(draws), shape[axis_at] // shards_of).reshape((-1,) + (1,) * (len(shape) - 1 - axis_at))
    return level


def gaussian(key, extent, spread, bound, cuts=(), kind=jnp.bfloat16):
    result = spread * jax.random.normal(key, extent, jnp.float32)
    if cuts:
        result = result * shard_levels(key, extent, cuts, -0.22, 0.18)
    return jnp.clip(result, -bound, bound).astype(kind)


def setup_inputs(seed: int = 0) -> dict:
    streams_of = jax.random.split(jax.random.key(seed), 5)
    queries = gaussian(streams_of[0], (TOKENS, HEADS * HEAD_DIM), 1.0, 6.0, ((0, 32),))
    keys = gaussian(streams_of[1], (TOKENS, HEADS * HEAD_DIM), 1.0, 6.0, ((0, 32),))
    values = gaussian(streams_of[2], (TOKENS, HEADS * HEAD_DIM), 1.0, 6.0, ((0, 32),))
    gain = jnp.clip(1.0 + 0.1 * jax.random.normal(streams_of[3], (HEADS * HEAD_DIM,), jnp.float32), 0.5, 1.5)
    return dict(queries=queries, keys=keys, values=values, gain=gain)


def reference(queries, keys, values, gain):
    nblocks = TOKENS // STRETCH
    q_all = queries.reshape(nblocks, STRETCH, HEADS, HEAD_DIM)
    k_all = keys.reshape(nblocks, STRETCH, HEADS, HEAD_DIM)
    v_all = values.reshape(nblocks, STRETCH, HEADS, HEAD_DIM)
    causal = jnp.arange(STRETCH)[:, None] >= jnp.arange(STRETCH)[None, :]
    gain_heads = gain.reshape(HEADS, HEAD_DIM)

    def step(carried, block):
        q_blk, k_blk, v_blk = block
        qf = q_blk.astype(jnp.float32)
        kf = k_blk.astype(jnp.float32)
        vf = v_blk.astype(jnp.float32)
        scores = jnp.einsum('qhd,khd->hqk', qf, kf)
        scores = jnp.where(causal[None], scores, 0.0).astype(jnp.bfloat16)
        carried_bf = carried.astype(jnp.bfloat16)
        raw = jnp.einsum('hqk,khd->qhd', scores.astype(jnp.float32), vf)
        raw = raw + jnp.einsum('qhd,hde->qhe', qf, carried_bf.astype(jnp.float32))
        scale = lax.rsqrt(lax.optimization_barrier(jnp.mean(raw * raw, axis=-1, keepdims=True)) + 1e-06)
        normed = (raw * scale * gain_heads[None]).astype(jnp.bfloat16)
        block_state = jnp.einsum('khd,khe->hde', kf, vf)
        return (carried + block_state, normed)
    start = jnp.zeros((HEADS, HEAD_DIM, HEAD_DIM), jnp.float32)
    final_state, outputs = lax.scan(step, start, (q_all, k_all, v_all))
    return outputs.reshape(TOKENS, HEADS * HEAD_DIM)
```

```python
import functools

import jax
import jax.numpy as jnp
from jax import lax
from jax.experimental import pallas as pl
from jax.experimental.pallas import tpu as pltpu
from jax.sharding import PartitionSpec as P

HEAD_DIM = 128
STRETCH = 128
AXES = ("outer", "inner")
CHUNKS = 2
F32 = jnp.float32
BF16 = jnp.bfloat16
D = HEAD_DIM


def vmem(shape, index):
    return pl.BlockSpec(shape, index)


def cols(head):
    start = head * D
    if isinstance(start, int):
        return pl.ds(start, D)
    return pl.ds(pl.multiple_of(start, D), D)


def states_body(ways, each, low_ref, k_ref, v_ref, *out_refs):
    low = low_ref[0]
    for r in range(ways):
        for j in range(each):
            at = cols((low ^ r) * each + j)
            out_refs[r][j] = lax.dot_general(
                k_ref[:, at], v_ref[:, at], (((0,), (0,)), ((), ())), preferred_element_type=F32
            )


def block_states(low, keys, values, ways, each, chunk, chunks):
    rows, width = keys.shape
    span = width // chunks
    spec = pl.BlockSpec((rows, span), lambda i, low: (0, chunk))
    piece = jax.ShapeDtypeStruct((each, D, D), F32)
    out_spec = pl.BlockSpec((each, D, D), lambda i, low: (0, 0, 0))
    return pl.pallas_call(
        functools.partial(states_body, ways, each),
        grid_spec=pltpu.PrefetchScalarGridSpec(
            num_scalar_prefetch=1, grid=(1,), in_specs=[spec, spec], out_specs=[out_spec] * ways
        ),
        out_shape=[piece] * ways,
        cost_estimate=pl.CostEstimate(
            flops=2 * rows * D * span, bytes_accessed=rows * span * 4 + span * D * 4, transcendentals=0
        ),
        name="block_states",
    )(low, keys, values)


def within_body(heads, q_ref, k_ref, v_ref, out_ref):
    rows = q_ref.shape[0]
    keep = lax.broadcasted_iota(jnp.int32, (rows, rows), 0) >= lax.broadcasted_iota(jnp.int32, (rows, rows), 1)
    for h in range(heads):
        at = cols(h)
        scores = lax.dot_general(
            q_ref[:, at], k_ref[:, at], (((1,), (1,)), ((), ())), preferred_element_type=F32
        )
        scores = jnp.where(keep, scores, 0.0).astype(BF16)
        out_ref[:, at] = jnp.dot(scores, v_ref[:, at], preferred_element_type=F32)


def within_block(queries, keys, values):
    rows, width = queries.shape
    spec = pl.BlockSpec((rows, width), lambda i: (0, 0))
    return pl.pallas_call(
        functools.partial(within_body, width // D),
        grid=(1,),
        in_specs=[spec] * 3,
        out_specs=spec,
        out_shape=jax.ShapeDtypeStruct((rows, width), F32),
        cost_estimate=pl.CostEstimate(
            flops=4 * rows * rows * width, bytes_accessed=rows * width * 10, transcendentals=0
        ),
        name="within_block",
    )(queries, keys, values)


def finish_body(ways, each, n_prev, low_ref, q_ref, near_ref, gain_ref, *refs):
    state_refs, out_ref = refs[:ways], refs[-1]
    low = low_ref[0]
    for s in range(ways):
        for j in range(each):
            at = cols((low ^ s) * each + j)
            raw = near_ref[:, at] + jnp.dot(
                q_ref[:, at], state_refs[s][j].astype(BF16), preferred_element_type=F32
            )
            scale = lax.rsqrt(jnp.mean(raw * raw, axis=-1, keepdims=True) + 1e-06)
            out_ref[:, at] = (raw * scale * gain_ref[:, at]).astype(BF16)


def finish(low, queries, near, gain, states, each, chunk, chunks, out):
    rows, width = queries.shape
    ways = len(states)
    span = width // chunks
    spec = pl.BlockSpec((rows, span), lambda i, low: (0, chunk))
    gain_spec = pl.BlockSpec((1, span), lambda i, low: (0, chunk))
    piece = pl.BlockSpec((each, D, D), lambda i, low: (0, 0, 0))
    extra = [] if out is None else [out]
    return pl.pallas_call(
        functools.partial(finish_body, ways, each, len(extra)),
        grid_spec=pltpu.PrefetchScalarGridSpec(
            num_scalar_prefetch=1,
            grid=(1,),
            in_specs=[spec, spec, gain_spec] + [piece] * ways + [pl.BlockSpec(memory_space=pl.ANY)] * len(extra),
            out_specs=spec,
        ),
        out_shape=jax.ShapeDtypeStruct((rows, width), BF16),
        input_output_aliases={} if out is None else {4 + ways: 0},
        cost_estimate=pl.CostEstimate(
            flops=2 * rows * D * span, bytes_accessed=rows * span * 8 + span * D * 4, transcendentals=rows * span // D
        ),
        name="finish",
    )(low, queries, near, gain, *states, *extra)


def on_device(size, queries, keys, values, gain):
    rows, width = queries.shape
    heads = width // D
    ways = 4
    chunks = CHUNKS
    each = heads // chunks // ways
    rank = lax.axis_index(AXES)
    low = rank % ways
    low_arr = jnp.full((1,), low, jnp.int32)

    def flip(value, mask):
        return lax.ppermute(value, AXES, [(d, d ^ mask) for d in range(size)])

    bits = []
    bit = ways
    while bit < size:
        bits.append(bit)
        bit *= 2

    own = [block_states(low_arr, keys, values, ways, each, c, chunks) for c in range(chunks)]
    near = within_block(queries, keys, values)
    gain = gain.reshape(1, width)
    got = [[own[c][0]] + [flip(own[c][r], r) for r in range(1, ways)] for c in range(chunks)]
    out = None
    finals = []
    for c in range(chunks):
        pieces = got[c]
        total = functools.reduce(jnp.add, pieces)
        before = jnp.zeros_like(total)
        for b in bits:
            if b == bits[-1]:
                other = lax.ppermute(total, AXES, [(d, d + b) for d in range(size) if d & b == 0])
                before = before + other
            else:
                other = flip(total, b)
                before = before + jnp.where(rank & b != 0, other, 0.0)
                total = total + other
        carried = []
        for s in range(ways):
            part = before
            for r in range(ways):
                if r != s:
                    part = part + jnp.where((low ^ r) < (low ^ s), pieces[r], 0.0)
            carried.append(part)
        finals.append([carried[0]] + [flip(carried[s], s) for s in range(1, ways)])
    for c in range(chunks):
        out = finish(low_arr, queries, near, gain, finals[c], each, c, chunks, out)
    return out


def solution(mesh):
    size = mesh.shape["outer"] * mesh.shape["inner"]
    return jax.shard_map(
        functools.partial(on_device, size),
        mesh=mesh,
        in_specs=(P(AXES, None), P(AXES, None), P(AXES, None), P()),
        out_specs=P(AXES, None),
        check_vma=False,
    )
```

```python
import functools

import jax
import jax.numpy as jnp
from jax import lax
from jax.experimental import pallas as pl
from jax.experimental.pallas import tpu as pltpu
from jax.sharding import PartitionSpec as P

D = 128
WAYS = 4
CHUNKS = 2
AXES = ("outer", "inner")
F32 = jnp.float32
BF16 = jnp.bfloat16
SMALL = pltpu.CompilerParams(vmem_limit_bytes=8 << 20)


def cost(flops, moved):
    return pl.CostEstimate(flops=flops, bytes_accessed=moved, transcendentals=0)


def first_body(each, place, slot, low_ref, k_hbm, v_hbm, out_ref, k_buf, v_buf, sems):
    block = slot * WAYS + (low_ref[0] ^ place)
    span = each * D
    at = pl.ds(pl.multiple_of(block * span, span), span)
    copies = [
        pltpu.make_async_copy(k_hbm.at[:, at], k_buf, sems.at[0]),
        pltpu.make_async_copy(v_hbm.at[:, at], v_buf, sems.at[1]),
    ]
    for copy in copies:
        copy.start()
    for copy in copies:
        copy.wait()
    for j in range(each):
        col = pl.ds(j * D, D)
        out_ref[j] = lax.dot_general(
            k_buf[:, col], v_buf[:, col], (((0,), (0,)), ((), ())), preferred_element_type=F32
        )


def first_state(low, keys, values, each, place, slot):
    rows = keys.shape[0]
    span = each * D
    return pl.pallas_call(
        functools.partial(first_body, each, place, slot),
        grid_spec=pltpu.PrefetchScalarGridSpec(
            num_scalar_prefetch=1,
            grid=(1,),
            in_specs=[pl.BlockSpec(memory_space=pltpu.HBM)] * 2,
            out_specs=pl.BlockSpec((each, D, D), lambda i, low: (0, 0, 0)),
            scratch_shapes=[
                pltpu.VMEM((rows, span), BF16),
                pltpu.VMEM((rows, span), BF16),
                pltpu.SemaphoreType.DMA((2,)),
            ],
        ),
        out_shape=jax.ShapeDtypeStruct((each, D, D), F32),
        cost_estimate=cost(2 * rows * D * span, rows * span * 4 + span * D * 4),
        compiler_params=SMALL,
        name="first_state",
    )(low, keys, values)


def states_body(each, places, low_ref, k_ref, v_ref, *out_refs):
    low = low_ref[0]
    span = each * D
    for out_ref, place in zip(out_refs, places):
        for j in range(each):
            at = pl.ds(pl.multiple_of((low ^ place) * span + j * D, D), D)
            out_ref[j] = lax.dot_general(
                k_ref[:, at], v_ref[:, at], (((0,), (0,)), ((), ())), preferred_element_type=F32
            )


def block_states(low, keys, values, each, places, slot):
    rows = keys.shape[0]
    span = each * D * WAYS
    spec = pl.BlockSpec((rows, span), lambda i, low: (0, slot))
    return pl.pallas_call(
        functools.partial(states_body, each, places),
        grid_spec=pltpu.PrefetchScalarGridSpec(
            num_scalar_prefetch=1,
            grid=(1,),
            in_specs=[spec, spec],
            out_specs=[pl.BlockSpec((each, D, D), lambda i, low: (0, 0, 0))] * len(places),
        ),
        out_shape=[jax.ShapeDtypeStruct((each, D, D), F32)] * len(places),
        cost_estimate=cost(2 * rows * D * span, rows * span * 4 + span * D * 4),
        compiler_params=SMALL,
        name="block_states",
    )(low, keys, values)


def within_body(heads, q_ref, k_ref, v_ref, out_ref):
    rows = q_ref.shape[0]
    keep = lax.broadcasted_iota(jnp.int32, (rows, rows), 0) >= lax.broadcasted_iota(jnp.int32, (rows, rows), 1)
    for h in range(heads):
        at = pl.ds(h * D, D)
        scores = lax.dot_general(
            q_ref[:, at], k_ref[:, at], (((1,), (1,)), ((), ())), preferred_element_type=F32
        )
        scores = jnp.where(keep, scores, 0.0).astype(BF16)
        out_ref[:, at] = jnp.dot(scores, v_ref[:, at], preferred_element_type=F32)


def within_block(queries, keys, values, slot, slots):
    rows, width = queries.shape
    span = width // slots
    spec = pl.BlockSpec((rows, span), lambda i: (0, slot))
    return pl.pallas_call(
        functools.partial(within_body, span // D),
        grid=(1,),
        in_specs=[spec] * 3,
        out_specs=pl.BlockSpec((rows, span), lambda i: (0, 0)),
        out_shape=jax.ShapeDtypeStruct((rows, span), F32),
        cost_estimate=cost(4 * rows * rows * span, rows * span * 10),
        compiler_params=SMALL,
        name="within_block",
    )(queries, keys, values)


def finish_body(each, places, low_ref, q_ref, near_ref, gain_ref, *refs):
    state_refs, out_ref = refs[: len(places)], refs[-1]
    low = low_ref[0]
    span = each * D
    for place, state_ref in zip(places, state_refs):
        for j in range(each):
            at = pl.ds(pl.multiple_of((low ^ place) * span + j * D, D), D)
            raw = near_ref[:, at] + jnp.dot(q_ref[:, at], state_ref[j].astype(BF16), preferred_element_type=F32)
            scale = lax.rsqrt(jnp.mean(raw * raw, axis=-1, keepdims=True) + 1e-06)
            out_ref[:, at] = (raw * scale * gain_ref[:, at]).astype(BF16)


def finish(low, queries, near, gain, states, each, slot, out):
    rows, width = queries.shape
    span = each * D * WAYS
    spec = pl.BlockSpec((rows, span), lambda i, low: (0, slot))
    extra = [] if out is None else [out]
    return pl.pallas_call(
        lambda *refs: finish_body(each, tuple(range(WAYS)), *refs[: 4 + WAYS], refs[-1]),
        grid_spec=pltpu.PrefetchScalarGridSpec(
            num_scalar_prefetch=1,
            grid=(1,),
            in_specs=[
                spec,
                pl.BlockSpec((rows, span), lambda i, low: (0, 0)),
                pl.BlockSpec((1, span), lambda i, low: (0, slot)),
            ]
            + [pl.BlockSpec((each, D, D), lambda i, low: (0, 0, 0))] * WAYS
            + [pl.BlockSpec(memory_space=pl.ANY)] * len(extra),
            out_specs=spec,
        ),
        out_shape=jax.ShapeDtypeStruct((rows, width), BF16),
        input_output_aliases={} if out is None else {4 + WAYS: 0},
        cost_estimate=cost(2 * rows * D * span, rows * span * 8 + span * D * 4),
        compiler_params=SMALL,
        name="finish",
    )(low, queries, near, gain, *states, *extra)


ORDER = (1, 3, 2)


def on_device(size, queries, keys, values, gain):
    _, width = queries.shape
    each = width // D // CHUNKS // WAYS
    rank = lax.axis_index(AXES)
    low = rank % WAYS
    low_arr = jnp.full((1,), low, jnp.int32)
    gain = gain.reshape(1, width)
    bits = [1 << b for b in range(2, size.bit_length() - 1)]

    def flip(value, mask):
        return lax.ppermute(value, AXES, [(d, d ^ mask) for d in range(size)])

    finals = []
    near = []
    for c in range(CHUNKS):
        own = {}
        rest = ORDER + (0,)
        if c == 0:
            own[1] = first_state(low_arr, keys, values, each, 1, c)
            rest = (3, 2, 0)
        for place, state in zip(rest, block_states(low_arr, keys, values, each, rest, c)):
            own[place] = state
        near.append(within_block(queries, keys, values, c, CHUNKS))
        pieces = {0: own[0]}
        for r in ORDER:
            pieces[r] = flip(own[r], r)
        total = functools.reduce(jnp.add, [pieces[r] for r in range(WAYS)])
        before = jnp.zeros_like(total)
        for b in bits:
            other = flip(total, b)
            before = before + jnp.where(rank & b != 0, other, 0.0)
            total = total + other
        carried = []
        for s in range(WAYS):
            part = before
            for r in range(WAYS):
                if r != s:
                    part = part + jnp.where((low ^ r) < (low ^ s), pieces[r], 0.0)
            carried.append(part)
        got = {0: carried[0]}
        for s in ORDER:
            got[s] = flip(carried[s], s)
        finals.append([got[s] for s in range(WAYS)])
    out = None
    for c in range(CHUNKS):
        out = finish(low_arr, queries, near[c], gain, finals[c], each, c, out)
    return out


def solution(mesh):
    size = mesh.shape["outer"] * mesh.shape["inner"]

    def body(*args):
        return on_device(size, *args)

    return jax.shard_map(
        body,
        mesh=mesh,
        in_specs=(P(AXES, None), P(AXES, None), P(AXES, None), P()),
        out_specs=P(AXES, None),
        check_vma=False,
    )
```

```python
import functools

import jax
import jax.numpy as jnp
from jax import lax
from jax.experimental import pallas as pl
from jax.experimental.pallas import tpu as pltpu
from jax.sharding import PartitionSpec as P

D = 128
WAYS = 4
COUNTS = (8, 8)
AXES = ("outer", "inner")
F32 = jnp.float32
BF16 = jnp.bfloat16
SMALL = pltpu.CompilerParams(vmem_limit_bytes=8 << 20)


def cost(flops, moved):
    return pl.CostEstimate(flops=flops, bytes_accessed=moved, transcendentals=0)


def emit_states(place_rows, heads, base, low, k_ref, v_ref, whole_ref, out_refs):
    for j in range(heads):
        at = pl.ds(base + j * D, D)
        whole_ref[j] = lax.dot_general(
            k_ref[:, at], v_ref[:, at], (((0,), (0,)), ((), ())), preferred_element_type=F32
        )
        for place, out_ref in enumerate(out_refs):
            start = pl.multiple_of((low ^ place) * place_rows, place_rows)
            out_ref[j] = whole_ref[j, pl.ds(start, place_rows), :]


def first_body(heads, low_ref, k_hbm, v_hbm, *refs):
    out_refs, (k_buf, v_buf, whole_ref, sems) = refs[:WAYS], refs[WAYS:]
    at = pl.ds(0, heads * D)
    copies = [
        pltpu.make_async_copy(k_hbm.at[:, at], k_buf, sems.at[0]),
        pltpu.make_async_copy(v_hbm.at[:, at], v_buf, sems.at[1]),
    ]
    for copy in copies:
        copy.start()
    for copy in copies:
        copy.wait()
    emit_states(D // WAYS, heads, 0, low_ref[0], k_buf, v_buf, whole_ref, out_refs)


def first_states(low, keys, values, heads):
    rows = keys.shape[0]
    shape = (heads, D // WAYS, D)
    return pl.pallas_call(
        functools.partial(first_body, heads),
        grid_spec=pltpu.PrefetchScalarGridSpec(
            num_scalar_prefetch=1,
            grid=(1,),
            in_specs=[pl.BlockSpec(memory_space=pltpu.HBM)] * 2,
            out_specs=[pl.BlockSpec(shape, lambda i, low: (0, 0, 0))] * WAYS,
            scratch_shapes=[
                pltpu.VMEM((rows, heads * D), BF16),
                pltpu.VMEM((rows, heads * D), BF16),
                pltpu.VMEM((heads, D, D), F32),
                pltpu.SemaphoreType.DMA((2,)),
            ],
        ),
        out_shape=[jax.ShapeDtypeStruct(shape, F32)] * WAYS,
        cost_estimate=cost(2 * rows * D * D * heads, rows * D * heads * 4 + heads * D * D * 4),
        compiler_params=SMALL,
        name="first_states",
    )(low, keys, values)


def states_body(counts, skip, low_ref, k_ref, v_ref, *refs):
    out_refs, whole_ref = refs[:-1], refs[-1]
    base = skip
    for i, heads in enumerate(counts):
        emit_states(
            D // WAYS, heads, base * D, low_ref[0], k_ref, v_ref, whole_ref, out_refs[i * WAYS : (i + 1) * WAYS]
        )
        base += heads


def block_states(low, keys, values, counts, skip):
    rows, width = keys.shape
    heads = sum(counts)
    shapes = [(n, D // WAYS, D) for n in counts for _ in range(WAYS)]
    spec = pl.BlockSpec((rows, width), lambda i, low: (0, 0))
    return pl.pallas_call(
        functools.partial(states_body, counts, skip),
        grid_spec=pltpu.PrefetchScalarGridSpec(
            num_scalar_prefetch=1,
            grid=(1,),
            in_specs=[spec, spec],
            out_specs=[pl.BlockSpec(shape, lambda i, low: (0, 0, 0)) for shape in shapes],
            scratch_shapes=[pltpu.VMEM((max(counts), D, D), F32)],
        ),
        out_shape=[jax.ShapeDtypeStruct(shape, F32) for shape in shapes],
        cost_estimate=cost(2 * rows * D * D * heads, rows * D * heads * 4 + heads * D * D * 4),
        compiler_params=SMALL,
        name="block_states",
    )(low, keys, values)


def within_body(heads, low_ref, q_ref, k_ref, v_ref, out_ref, turned_ref):
    rows = q_ref.shape[0]
    row = lax.broadcasted_iota(jnp.int32, (rows, rows), 0)
    keep = row >= lax.broadcasted_iota(jnp.int32, (rows, rows), 1)
    lane = lax.broadcasted_iota(jnp.int32, (D, D), 1)
    place_rows = D // WAYS
    source = ((lane // place_rows) ^ low_ref[0]) * place_rows + lane % place_rows
    turn = jnp.where(lax.broadcasted_iota(jnp.int32, (D, D), 0) == source, 1.0, 0.0).astype(BF16)
    for h in range(heads):
        at = pl.ds(h * D, D)
        scores = lax.dot_general(
            q_ref[:, at], k_ref[:, at], (((1,), (1,)), ((), ())), preferred_element_type=F32
        )
        scores = jnp.where(keep, scores, 0.0).astype(BF16)
        out_ref[:, at] = jnp.dot(scores, v_ref[:, at], preferred_element_type=F32)
        turned_ref[:, at] = jnp.dot(q_ref[:, at], turn, preferred_element_type=F32).astype(BF16)


def within_block(low, queries, keys, values):
    rows, width = queries.shape
    spec = pl.BlockSpec((rows, width), lambda i, low: (0, 0))
    return pl.pallas_call(
        functools.partial(within_body, width // D),
        grid_spec=pltpu.PrefetchScalarGridSpec(
            num_scalar_prefetch=1, grid=(1,), in_specs=[spec] * 3, out_specs=[spec] * 2
        ),
        out_shape=[jax.ShapeDtypeStruct((rows, width), F32), jax.ShapeDtypeStruct((rows, width), BF16)],
        cost_estimate=cost(6 * rows * rows * width, rows * width * 12),
        compiler_params=SMALL,
        name="within_block",
    )(low, queries, keys, values)


def finish_body(heads, base, q_ref, near_ref, gain_ref, *refs):
    state_refs, (out_hbm, block, sem) = refs[:WAYS], refs[-3:]
    for j in range(heads):
        state = jnp.concatenate([ref[j] for ref in state_refs], axis=0).astype(BF16)
        at = pl.ds((base + j) * D, D)
        raw = near_ref[:, at] + jnp.dot(q_ref[:, at], state, preferred_element_type=F32)
        scale = lax.rsqrt(jnp.mean(raw * raw, axis=-1, keepdims=True) + 1e-06)
        block[:, pl.ds(j * D, D)] = (raw * scale * gain_ref[:, at]).astype(BF16)
    copy = pltpu.make_async_copy(block, out_hbm.at[:, pl.ds(base * D, heads * D)], sem)
    copy.start()
    copy.wait()


def finish(turned, near, gain, states, heads, base, out):
    rows, width = turned.shape
    spec = pl.BlockSpec(memory_space=pltpu.VMEM)
    extra = [] if out is None else [out]
    return pl.pallas_call(
        functools.partial(finish_body, heads, base),
        in_specs=[spec] * 3
        + [spec] * WAYS
        + [pl.BlockSpec(memory_space=pltpu.HBM)] * len(extra),
        out_specs=pl.BlockSpec(memory_space=pltpu.HBM),
        scratch_shapes=[pltpu.VMEM((rows, heads * D), BF16), pltpu.SemaphoreType.DMA],
        out_shape=jax.ShapeDtypeStruct((rows, width), BF16),
        input_output_aliases={} if out is None else {3 + WAYS: 0},
        cost_estimate=cost(2 * rows * D * D * heads, rows * D * heads * 8 + heads * D * D * 4),
        compiler_params=SMALL,
        name="finish",
    )(turned, near, gain, *states, *extra)


ORDER = (1, 3, 2)


def on_device(size, queries, keys, values, gain):
    _, width = queries.shape
    rank = lax.axis_index(AXES)
    low = rank % WAYS
    low_arr = jnp.full((1,), low, jnp.int32)
    gain = gain.reshape(1, width)
    bits = [1 << b for b in range(2, size.bit_length() - 1)]

    def flip(value, mask):
        return lax.ppermute(value, AXES, [(d, d ^ mask) for d in range(size)])

    finals = []
    first = first_states(
        low_arr,
        pltpu.with_memory_space_constraint(keys, pltpu.HBM),
        pltpu.with_memory_space_constraint(values, pltpu.HBM),
        COUNTS[0],
    )
    rest = block_states(low_arr, keys, values, COUNTS[1:], COUNTS[0])
    states = list(first) + list(rest)
    near, turned = within_block(low_arr, queries, keys, values)
    for c in range(len(COUNTS)):
        own = states[c * WAYS : (c + 1) * WAYS]
        pieces = {0: own[0]}
        for r in ORDER:
            pieces[r] = flip(own[r], r)
        total = functools.reduce(jnp.add, [pieces[r] for r in range(WAYS)])
        before = jnp.zeros_like(total)
        for b in bits:
            other = flip(total, b)
            before = before + jnp.where(rank & b != 0, other, 0.0)
            total = total + other
        carried = []
        for s in range(WAYS):
            part = before
            for r in range(WAYS):
                if r != s:
                    part = part + jnp.where((low ^ r) < (low ^ s), pieces[r], 0.0)
            carried.append(part)
        got = {0: carried[0]}
        for s in ORDER:
            got[s] = flip(carried[s], s)
        finals.append([got[s] for s in range(WAYS)])
    out = None
    for c, heads in enumerate(COUNTS):
        out = finish(turned, near, gain, finals[c], heads, sum(COUNTS[:c]), out)
    return out


def solution(mesh):
    size = mesh.shape["outer"] * mesh.shape["inner"]

    def body(*args):
        return on_device(size, *args)

    return jax.shard_map(
        body,
        mesh=mesh,
        in_specs=(P(AXES, None), P(AXES, None), P(AXES, None), P()),
        out_specs=P(AXES, None),
        check_vma=False,
    )
```

```python
import functools

import jax
import jax.numpy as jnp
from jax import lax
from jax.experimental import pallas as pl
from jax.experimental.pallas import tpu as pltpu
from jax.sharding import PartitionSpec as P

D = 128
WAYS = 4
COUNTS = (8, 8)
AXES = ("outer", "inner")
F32 = jnp.float32
BF16 = jnp.bfloat16
SMALL = pltpu.CompilerParams(vmem_limit_bytes=8 << 20)


def cost(flops, moved):
    return pl.CostEstimate(flops=flops, bytes_accessed=moved, transcendentals=0)


def emit_states(place_rows, heads, base, low, k_ref, v_ref, whole_ref, out_refs):
    for j in range(heads):
        at = pl.ds(base + j * D, D)
        whole_ref[j] = lax.dot_general(
            k_ref[:, at], v_ref[:, at], (((0,), (0,)), ((), ())), preferred_element_type=F32
        )
        for place, out_ref in enumerate(out_refs):
            start = pl.multiple_of((low ^ place) * place_rows, place_rows)
            out_ref[j] = whole_ref[j, pl.ds(start, place_rows), :]


def first_body(heads, low_ref, k_hbm, v_hbm, *refs):
    out_refs, (k_buf, v_buf, whole_ref, sems) = refs[:WAYS], refs[WAYS:]
    at = pl.ds(0, heads * D)
    copies = [
        pltpu.make_async_copy(k_hbm.at[:, at], k_buf, sems.at[0]),
        pltpu.make_async_copy(v_hbm.at[:, at], v_buf, sems.at[1]),
    ]
    for copy in copies:
        copy.start()
    for copy in copies:
        copy.wait()
    emit_states(D // WAYS, heads, 0, low_ref[0], k_buf, v_buf, whole_ref, out_refs)


def first_states(low, keys, values, heads):
    rows = keys.shape[0]
    shape = (heads, D // WAYS, D)
    return pl.pallas_call(
        functools.partial(first_body, heads),
        grid_spec=pltpu.PrefetchScalarGridSpec(
            num_scalar_prefetch=1,
            grid=(1,),
            in_specs=[pl.BlockSpec(memory_space=pltpu.HBM)] * 2,
            out_specs=[pl.BlockSpec(shape, lambda i, low: (0, 0, 0))] * WAYS,
            scratch_shapes=[
                pltpu.VMEM((rows, heads * D), BF16),
                pltpu.VMEM((rows, heads * D), BF16),
                pltpu.VMEM((heads, D, D), F32),
                pltpu.SemaphoreType.DMA((2,)),
            ],
        ),
        out_shape=[jax.ShapeDtypeStruct(shape, F32)] * WAYS,
        cost_estimate=cost(2 * rows * D * D * heads, rows * D * heads * 4 + heads * D * D * 4),
        compiler_params=SMALL,
        name="first_states",
    )(low, keys, values)


def states_body(counts, skip, low_ref, k_ref, v_ref, *refs):
    out_refs, whole_ref = refs[:-1], refs[-1]
    base = skip
    for i, heads in enumerate(counts):
        emit_states(
            D // WAYS, heads, base * D, low_ref[0], k_ref, v_ref, whole_ref, out_refs[i * WAYS : (i + 1) * WAYS]
        )
        base += heads


def block_states(low, keys, values, counts, skip):
    rows, width = keys.shape
    heads = sum(counts)
    shapes = [(n, D // WAYS, D) for n in counts for _ in range(WAYS)]
    spec = pl.BlockSpec((rows, width), lambda i, low: (0, 0))
    return pl.pallas_call(
        functools.partial(states_body, counts, skip),
        grid_spec=pltpu.PrefetchScalarGridSpec(
            num_scalar_prefetch=1,
            grid=(1,),
            in_specs=[spec, spec],
            out_specs=[pl.BlockSpec(shape, lambda i, low: (0, 0, 0)) for shape in shapes],
            scratch_shapes=[pltpu.VMEM((max(counts), D, D), F32)],
        ),
        out_shape=[jax.ShapeDtypeStruct(shape, F32) for shape in shapes],
        cost_estimate=cost(2 * rows * D * D * heads, rows * D * heads * 4 + heads * D * D * 4),
        compiler_params=SMALL,
        name="block_states",
    )(low, keys, values)


def within_body(heads, low_ref, q_ref, k_ref, v_ref, out_ref, turned_ref):
    rows = q_ref.shape[0]
    row = lax.broadcasted_iota(jnp.int32, (rows, rows), 0)
    keep = row >= lax.broadcasted_iota(jnp.int32, (rows, rows), 1)
    lane = lax.broadcasted_iota(jnp.int32, (D, D), 1)
    place_rows = D // WAYS
    source = ((lane // place_rows) ^ low_ref[0]) * place_rows + lane % place_rows
    turn = jnp.where(lax.broadcasted_iota(jnp.int32, (D, D), 0) == source, 1.0, 0.0).astype(BF16)
    for h in range(heads):
        at = pl.ds(h * D, D)
        scores = lax.dot_general(
            q_ref[:, at], k_ref[:, at], (((1,), (1,)), ((), ())), preferred_element_type=F32
        )
        scores = jnp.where(keep, scores, 0.0).astype(BF16)
        out_ref[:, at] = jnp.dot(scores, v_ref[:, at], preferred_element_type=F32)
        turned_ref[:, at] = jnp.dot(q_ref[:, at], turn, preferred_element_type=F32).astype(BF16)


def within_block(low, queries, keys, values):
    rows, width = queries.shape
    spec = pl.BlockSpec((rows, width), lambda i, low: (0, 0))
    return pl.pallas_call(
        functools.partial(within_body, width // D),
        grid_spec=pltpu.PrefetchScalarGridSpec(
            num_scalar_prefetch=1, grid=(1,), in_specs=[spec] * 3, out_specs=[spec] * 2
        ),
        out_shape=[jax.ShapeDtypeStruct((rows, width), F32), jax.ShapeDtypeStruct((rows, width), BF16)],
        cost_estimate=cost(6 * rows * rows * width, rows * width * 12),
        compiler_params=SMALL,
        name="within_block",
    )(low, queries, keys, values)


def finish_body(heads, base, q_ref, near_ref, gain_ref, *refs):
    state_refs, (out_hbm, block, sem) = refs[:WAYS], refs[-3:]
    for j in range(heads):
        state = jnp.concatenate([ref[j] for ref in state_refs], axis=0).astype(BF16)
        at = pl.ds((base + j) * D, D)
        raw = near_ref[:, at] + jnp.dot(q_ref[:, at], state, preferred_element_type=F32)
        scale = lax.rsqrt(jnp.mean(raw * raw, axis=-1, keepdims=True) + 1e-06)
        block[:, pl.ds(j * D, D)] = (raw * scale * gain_ref[:, at]).astype(BF16)
    copy = pltpu.make_async_copy(block, out_hbm.at[:, pl.ds(base * D, heads * D)], sem)
    copy.start()
    copy.wait()


def finish(turned, near, gain, states, heads, base, out):
    rows, width = turned.shape
    spec = pl.BlockSpec(memory_space=pltpu.VMEM)
    extra = [] if out is None else [out]
    return pl.pallas_call(
        functools.partial(finish_body, heads, base),
        in_specs=[spec] * 3
        + [spec] * WAYS
        + [pl.BlockSpec(memory_space=pltpu.HBM)] * len(extra),
        out_specs=pl.BlockSpec(memory_space=pltpu.HBM),
        scratch_shapes=[pltpu.VMEM((rows, heads * D), BF16), pltpu.SemaphoreType.DMA],
        out_shape=jax.ShapeDtypeStruct((rows, width), BF16),
        input_output_aliases={} if out is None else {3 + WAYS: 0},
        cost_estimate=cost(2 * rows * D * D * heads, rows * D * heads * 8 + heads * D * D * 4),
        compiler_params=SMALL,
        name="finish",
    )(turned, near, gain, *states, *extra)


ORDER = (1, 3, 2)


def on_device(size, inner, queries, keys, values, gain):
    _, width = queries.shape
    rank = lax.axis_index(AXES)
    low = rank % WAYS
    low_arr = jnp.full((1,), low, jnp.int32)
    gain = gain.reshape(1, width)
    bits = [1 << b for b in range(2, size.bit_length() - 1)]

    def flip(value, mask):
        return lax.ppermute(value, AXES, [(d, d ^ mask) for d in range(size)])

    finals = []
    first = first_states(
        low_arr,
        pltpu.with_memory_space_constraint(keys, pltpu.HBM),
        pltpu.with_memory_space_constraint(values, pltpu.HBM),
        COUNTS[0],
    )
    rest = block_states(low_arr, keys, values, COUNTS[1:], COUNTS[0])
    states = list(first) + list(rest)
    near, turned = within_block(low_arr, queries, keys, values)
    for c in range(len(COUNTS)):
        own = states[c * WAYS : (c + 1) * WAYS]
        pieces = {0: own[0]}
        for r in ORDER:
            pieces[r] = flip(own[r], r)
        total = functools.reduce(jnp.add, [pieces[r] for r in range(WAYS)])
        before = jnp.zeros_like(total)
        for b in [b for b in bits if b < inner]:
            other = flip(total, b)
            before = before + jnp.where(rank & b != 0, other, 0.0)
            total = total + other
        group, earlier = total, jnp.zeros_like(total)
        for b in [b for b in bits if b > inner]:
            other = flip(total, b)
            earlier = earlier + jnp.where(rank & b != 0, other, 0.0)
            total = total + other
        other = flip(earlier + jnp.where(rank & inner != 0, 0.0, group), inner)
        before = before + earlier + other
        carried = []
        for s in range(WAYS):
            part = before
            for r in range(WAYS):
                if r != s:
                    part = part + jnp.where((low ^ r) < (low ^ s), pieces[r], 0.0)
            carried.append(part)
        got = {0: carried[0]}
        for s in ORDER:
            got[s] = flip(carried[s], s)
        finals.append([got[s] for s in range(WAYS)])
    out = None
    for c, heads in enumerate(COUNTS):
        out = finish(turned, near, gain, finals[c], heads, sum(COUNTS[:c]), out)
    return out


def solution(mesh):
    inner = mesh.shape["inner"]
    size = mesh.shape["outer"] * inner

    def body(*args):
        return on_device(size, inner, *args)

    return jax.shard_map(
        body,
        mesh=mesh,
        in_specs=(P(AXES, None), P(AXES, None), P(AXES, None), P()),
        out_specs=P(AXES, None),
        check_vma=False,
    )
```
